256 devices in a mesh: row: 8 (over z), col: 32 (over y, x, core).
Axes of the slice: x: 4, y: 4, z: 8, core: 2. Of those that a mesh axis runs over, the one named last changes fastest.
Arguments:
- inverse_first: float32 [512, 512], P('row'), may hold values from -0.4 to 2
- inverse_second: float32 [512, 512], P('row'), may hold values from -0.4 to 2
- coupling: float32 [512, 512], P('row'), may hold values from -0.25 to 0.25
- panel_first: float32 [32768, 512], P('row', 'col'), may hold values from -0.1875 to 0.1875
- panel_second: float32 [32768, 512], P('row', 'col'), may hold values from -0.1875 to 0.1875
- rhs_first: float32 [512, 8192], P('row', 'col'), may hold values from -6 to 6
- rhs_second: float32 [512, 8192], P('row', 'col'), may hold values from -6 to 6
- rhs_rest: float32 [32768, 8192], P('row', 'col'), may hold values from -6 to 6
Outputs:
- solved_first: float32 [512, 8192], P('row', 'col')
- solved_second: float32 [512, 8192], P('row', 'col')
- updated: float32 [32768, 8192], P('row', 'col')
The draws below stay inside these ranges and needn't reach their ends.
All inputs are finite; a program needn't handle non-finite values.
Results may differ from the reference program's by a relative error of at most 0.00011.
Values sent between devices are 32-bit elements; how exact they have to be, the bound alone decides.
A program may use at most 64 MiB of HBM per device.

```python
import math
import jax
import jax.numpy as jnp
from jax import lax

NB = 512
SAMPLES = 8192
REST = 32768


def lower_factor(key):
    key_off, key_diag = jax.random.split(key)
    rows = lax.broadcasted_iota(jnp.int32, (NB, NB), 0)
    cols = lax.broadcasted_iota(jnp.int32, (NB, NB), 1)
    offdiag = jnp.clip(jax.random.normal(key_off, (NB, NB), jnp.float32), -4.0, 4.0) * (0.6 / math.sqrt(NB))
    diag_vals = jax.random.uniform(key_diag, (NB,), jnp.float32, 0.7, 1.4)
    diag_full = jnp.broadcast_to(diag_vals[:, None], (NB, NB))
    zeros_full = jnp.zeros((NB, NB), jnp.float32)
    return jnp.where(rows > cols, offdiag, jnp.where(rows == cols, diag_full, zeros_full))


def draw_inverse_first(key, part):
    return lower_factor(jax.random.fold_in(key, 11))


def draw_inverse_second(key, part):
    return lower_factor(jax.random.fold_in(key, 23))


def block_levels(own_key, shape, shards, low, top_value):
    loudness = 1.0
    for position, parts in shards:
        steps = jax.random.uniform(jax.random.fold_in(jax.random.fold_in(own_key, 6), position), (parts,), jnp.float32, low / len(shards), top_value / len(shards))
        loudness = loudness * jnp.repeat(jnp.exp(steps), shape[position] // parts).reshape((-1,) + (1,) * (len(shape) - 1 - position))
    return loudness


def scatter_about(rng, extent, scale, most, cuts=(), kind=jnp.bfloat16):
    drawn = scale * jax.random.normal(rng, extent, jnp.float32)
    if cuts:
        drawn = drawn * block_levels(rng, extent, cuts, -0.22, 0.18)
    return jnp.clip(drawn, -most, most).astype(kind)


def setup_inputs(seed: int = 0) -> dict:
    keys = jax.random.split(jax.random.key(seed), 9)
    inverse_first = draw_inverse_first(jax.random.fold_in(keys[8], 71), 0)
    inverse_second = draw_inverse_second(jax.random.fold_in(keys[8], 71), 0)
    coupling = scatter_about(keys[2], (NB, NB), NB ** -0.5, 0.25, ((0, 8),), jnp.float32)
    panel_first = scatter_about(keys[3], (REST, NB), (2 * NB) ** -0.5, 0.1875, ((0, 8), (1, 32)), jnp.float32)
    panel_second = scatter_about(keys[4], (REST, NB), (2 * NB) ** -0.5, 0.1875, ((0, 8), (1, 32)), jnp.float32)
    rhs_first = scatter_about(keys[5], (NB, SAMPLES), 1.0, 6.0, ((0, 8), (1, 32)), jnp.float32)
    rhs_second = scatter_about(keys[6], (NB, SAMPLES), 1.0, 6.0, ((0, 8), (1, 32)), jnp.float32)
    rhs_rest = scatter_about(keys[7], (REST, SAMPLES), 1.0, 6.0, ((0, 8), (1, 32)), jnp.float32)
    return dict(inverse_first=inverse_first, inverse_second=inverse_second, coupling=coupling, panel_first=panel_first, panel_second=panel_second, rhs_first=rhs_first, rhs_second=rhs_second, rhs_rest=rhs_rest)


def product(left, right):
    return jnp.dot(left, right, precision=lax.Precision.HIGHEST, preferred_element_type=jnp.float32)


def reference(inverse_first, inverse_second, coupling, panel_first, panel_second, rhs_first, rhs_second, rhs_rest):
    solved_first = product(inverse_first, rhs_first)
    reduced = rhs_second - product(coupling, solved_first)
    solved_second = product(inverse_second, reduced)
    updated = rhs_rest - product(panel_first, solved_first) - product(panel_second, solved_second)
    return solved_first, solved_second, updated
```

```python
import functools

import jax
import jax.numpy as jnp
from jax import lax
from jax.experimental import pallas as pl
from jax.experimental.pallas import tpu as pltpu
from jax.sharding import PartitionSpec as P

MESH = pl.DeviceIdType.MESH
NG = 8
AHEAD = 2


def split(v):
    hi = v.astype(jnp.bfloat16)
    return hi, (v - hi.astype(jnp.float32)).astype(jnp.bfloat16)


def dot3(a, b):
    f = functools.partial(jnp.dot, preferred_element_type=jnp.float32)
    return f(a[0], b[0]) + (f(a[0], b[1]) + f(a[1], b[0]))


def kernel(
    a1, a2, cp, pt0, pt1, r1, r2, rest,
    out1, out2, upd,
    grid, zb1, zb2, xb1, xb2, sol, st,
    rsem, ssem, lsem, zrsem, zssem, zlsem, bsem,
):
    rows = pt0.shape[1] // NG
    z = lax.axis_index("row")
    col = lax.axis_index("col")
    y, x, h = col // 8, (col // 2) % 4, col % 2
    oh = 1 - h

    def cid(yy, xx, hh):
        return (yy * 4 + xx) * 2 + hh

    xp = (z, cid(y, (x + 1) % 4, h))
    xm = (z, cid(y, (x + 3) % 4, h))
    yp = (z, cid((y + 1) % 4, x, h))
    ym = (z, cid((y + 3) % 4, x, h))
    zp = ((z + 1) % 8, col)
    zm = ((z + 7) % 8, col)
    sib = (z, cid(y, x, oh))

    def send(src, dst, s, r, dev):
        pltpu.make_async_remote_copy(
            src_ref=src, dst_ref=dst, send_sem=s, recv_sem=r,
            device_id=dev, device_id_type=MESH,
        ).start()

    def take(ref, sem):
        pltpu.make_async_copy(ref, ref, sem).wait()

    panels = (
        (pt0, x, y, xp, xm, yp, ym),
        (pt1, y, x, yp, ym, xp, xm),
    )

    def local_own(g, p):
        pt, a, b = panels[p][:3]
        src = pt.at[:, pl.ds(pl.multiple_of(g * rows, rows), rows)]
        return pltpu.make_async_copy(src, grid.at[g, p, h, b, a], lsem.at[g, p])

    def stage_a(g):
        for p in range(2):
            pt, a, b, ap, am, bp, bm = panels[p]
            src = pt.at[:, pl.ds(pl.multiple_of(g * rows, rows), rows)]
            dst = grid.at[g, p, h, b, a]
            s = ssem.at[g, p]
            send(src, dst, s, rsem.at[g, p, 0], ap)
            send(src, dst, s, rsem.at[g, p, 1], am)
            send(src, dst, s, rsem.at[g, p, 3], bp)
            send(src, dst, s, rsem.at[g, p, 4], bm)

    def stage_b(g):
        for p in range(2):
            pt, a, b, ap, am, bp, bm = panels[p]
            s = ssem.at[g, p]
            for k, da, to, half in ((0, 3, ap, 0), (1, 1, am, 8)):
                ai = (a + da) % 4
                ref = grid.at[g, p, h, b, ai]
                take(ref, rsem.at[g, p, k])
                part = grid.at[g, p, h, b, ai, pl.ds(half, 8)]
                send(part, part, s, rsem.at[g, p, 2], to)
                send(ref, ref, s, rsem.at[g, p, 3], bp)
                send(ref, ref, s, rsem.at[g, p, 4], bm)

    def stage_c(g):
        for p in range(2):
            pt, a, b, ap, am, bp, bm = panels[p]
            s = ssem.at[g, p]
            ref = grid.at[g, p, h, b, (a + 2) % 4]
            take(ref, rsem.at[g, p, 2])
            send(ref, ref, s, rsem.at[g, p, 3], bp)
            send(ref, ref, s, rsem.at[g, p, 4], bm)
            local_own(g, p).wait()
            ref = grid.at[g, p, h, b]
            send(ref, ref, bsem.at[g, p], rsem.at[g, p, 6], sib)

    def stage_d(g):
        for p in range(2):
            pt, a, b, ap, am, bp, bm = panels[p]
            s = ssem.at[g, p]
            for k, db, to, half in ((3, 3, bp, 0), (4, 1, bm, 2)):
                bi = (b + db) % 4
                ref = grid.at[g, p, h, bi]
                take(ref, rsem.at[g, p, k])
                part = grid.at[g, p, h, bi, pl.ds(half, 2)]
                send(part, part, s, rsem.at[g, p, 5], to)
                send(ref, ref, bsem.at[g, p], rsem.at[g, p, 6], sib)

    def stage_e(g):
        for p in range(2):
            b = panels[p][2]
            ref = grid.at[g, p, h, (b + 2) % 4]
            take(ref, rsem.at[g, p, 5])
            send(ref, ref, bsem.at[g, p], rsem.at[g, p, 6], sib)

    def stage_f(g):
        acc = None
        for p in range(2):
            take(grid.at[g, p, oh], rsem.at[g, p, 6])
        for p in range(2):
            m = split(grid[g, p].reshape(32 * 16, rows))
            t = dot3((st[p, 0], st[p, 1]), m)
            acc = t if acc is None else acc + t
        here = pl.ds(pl.multiple_of(g * rows, rows), rows)
        upd[here, :] = upd[here, :] - acc.T

    mcols = pl.ds(pl.multiple_of(h * 256, 256), 256)
    batches = (
        (zb1, (r1, a1.at[:, mcols])),
        (zb2, (r2, cp.at[:, mcols], a2.at[:, mcols])),
    )

    def z_own(bt):
        zb, items = batches[bt]
        for i, src in enumerate(items):
            dst = zb.at[z, i]
            send(src, dst, zssem.at[bt], zrsem.at[bt, 0], zp)
            send(src, dst, zssem.at[bt], zrsem.at[bt, 3], zm)

    def z_local(bt):
        zb, items = batches[bt]
        return [
            pltpu.make_async_copy(src, zb.at[z, i], zlsem.at[bt, i])
            for i, src in enumerate(items)
        ]

    def z_hop(bt, k):
        zb = batches[bt][0]
        for d, to, half, at in ((8 - k, zp, 0, 0), (k, zm, 32, 3)):
            zi = (z + d) % 8
            ref = zb.at[zi]
            take(ref, zrsem.at[bt, at + k - 1])
            if k < 3:
                send(ref, ref, zssem.at[bt], zrsem.at[bt, at + k], to)
            else:
                part = zb.at[zi, :, pl.ds(half, 32)]
                send(part, part, zssem.at[bt], zrsem.at[bt, 6], to)

    def z_last(bt):
        zb = batches[bt][0]
        take(zb.at[(z + 4) % 8], zrsem.at[bt, 6])
        for c in z_local(bt):
            c.wait()
        if bt == 0:
            send(zb1.at[:, pl.ds(1, 1)], xb1, zssem.at[2], zrsem.at[0, 7], sib)
        else:
            send(zb2.at[:, pl.ds(1, 2)], xb2, zssem.at[3], zrsem.at[1, 7], sib)

    def apply(own, other, load):
        here = split(load(h).reshape(256, 256))
        there = split(load(oh).reshape(256, 256))
        return dot3(split(own.reshape(512, 256)), here) + dot3(
            split(other.reshape(512, 256)), there
        )

    def keep(p, s):
        order = [
            (o // 4 % 4 * 4 + o % 4) * 2 + o // 16 if p == 0
            else (o % 4 * 4 + o // 4 % 4) * 2 + o // 16
            for o in range(32)
        ]
        perm = jnp.concatenate([s[c * 16:c * 16 + 16] for c in order], axis=0)
        hi, lo = split(perm.T)
        st[p, 0] = hi
        st[p, 1] = lo

    def solve_first():
        take(xb1, zrsem.at[0, 7])
        s = apply(
            zb1[:, 1], xb1[:, 0], lambda q: zb1[pl.ds(q * 4, 4), 0]
        )
        sol[0] = s.reshape(8, 64, 256)
        out1[...] = sol[0, z]
        keep(0, s)

    def solve_second():
        take(xb2, zrsem.at[1, 7])
        red = zb2[:, 0].reshape(512, 256) - apply(
            zb2[:, 1], xb2[:, 0], lambda q: sol[0, pl.ds(q * 4, 4)]
        )
        sol[1] = red.reshape(8, 64, 256)
        s = apply(
            zb2[:, 2], xb2[:, 1], lambda q: sol[1, pl.ds(q * 4, 4)]
        )
        sol[1] = s.reshape(8, 64, 256)
        out2[...] = sol[1, z]
        keep(1, s)

    barrier = pltpu.get_barrier_semaphore()
    near = (xp, xm, yp, ym, zp, zm, sib)
    for dev in near:
        pl.semaphore_signal(barrier, inc=1, device_id=dev, device_id_type=MESH)
    pl.semaphore_wait(barrier, len(near))

    stage_a(0)
    z_own(0)
    for g in range(1, AHEAD + 1):
        stage_a(g)
    z_own(1)

    @pl.loop(0, NG)
    def _(g):
        for p in range(2):
            local_own(g, p).start()

    for bt in range(2):
        for c in z_local(bt):
            c.start()
    rest_copy = pltpu.make_async_copy(rest, upd, zlsem.at[0, 2])
    rest_copy.start()

    zplan = {
        0: (lambda: z_hop(0, 1),),
        1: (lambda: z_hop(0, 2), lambda: z_hop(1, 1)),
        2: (lambda: z_hop(0, 3), lambda: z_hop(1, 2)),
        3: (lambda: z_last(0), lambda: z_hop(1, 3)),
        4: (solve_first, lambda: z_last(1)),
        5: (solve_second, rest_copy.wait),
    }
    first = 5

    @pl.loop(0, NG + first)
    def _(t):
        @pl.when(t + AHEAD + 1 < NG)
        def _():
            stage_a(t + AHEAD + 1)

        for lag, stage in enumerate((stage_b, stage_c, stage_d, stage_e)):
            @pl.when((t >= lag) & (t < NG + lag))
            def _(lag=lag, stage=stage):
                stage(t - lag)

        for k, jobs in zplan.items():
            @pl.when(t == k)
            def _(jobs=jobs):
                for job in jobs:
                    job()

        @pl.when(t >= first)
        def _():
            stage_f(t - first)

    @pl.loop(0, NG)
    def _(g):
        for p in range(2):
            take(upd.at[pl.ds(0, 15 * rows // 16)], ssem.at[g, p])
            take(grid.at[g, p, h], bsem.at[g, p])

    take(zb1.at[pl.ds(0, 7)], zssem.at[0])
    take(zb2.at[pl.ds(0, 7)], zssem.at[1])
    take(xb1, zssem.at[2])
    take(xb2, zssem.at[3])


def per_device(
    inverse_first,
    inverse_second,
    coupling,
    panel_first,
    panel_second,
    rhs_first,
    rhs_second,
    rhs_rest,
):
    rows = rhs_rest.shape[0]
    f32 = jnp.float32
    group = rows // NG
    any_spec = pl.BlockSpec(memory_space=pl.ANY)
    vmem_spec = pl.BlockSpec(memory_space=pltpu.VMEM)
    sem = pltpu.SemaphoreType.DMA
    return pl.pallas_call(
        kernel,
        out_shape=(
            jax.ShapeDtypeStruct((64, 256), f32),
            jax.ShapeDtypeStruct((64, 256), f32),
            jax.ShapeDtypeStruct((rows, 256), f32),
        ),
        in_specs=[any_spec] * 8,
        out_specs=(vmem_spec,) * 3,
        scratch_shapes=[
            pltpu.VMEM((NG, 2, 2, 4, 4, 16, group), f32),
            pltpu.VMEM((8, 2, 64, 256), f32),
            pltpu.VMEM((8, 3, 64, 256), f32),
            pltpu.VMEM((8, 1, 64, 256), f32),
            pltpu.VMEM((8, 2, 64, 256), f32),
            pltpu.VMEM((2, 8, 64, 256), f32),
            pltpu.VMEM((2, 2, 256, 512), jnp.bfloat16),
            sem((NG, 2, 7)),
            sem((NG, 2)),
            sem((NG, 2)),
            sem((2, 8)),
            sem((4,)),
            sem((2, 3)),
            sem((NG, 2)),
        ],
        compiler_params=pltpu.CompilerParams(
            collective_id=0, has_side_effects=True, vmem_limit_bytes=48 * 1024 * 1024
        ),
    )(
        inverse_first,
        inverse_second,
        coupling,
        panel_first.T,
        panel_second.T,
        rhs_first,
        rhs_second,
        rhs_rest,
    )


def solution(mesh):
    in_specs = (
        P("row", None),
        P("row", None),
        P("row", None),
        P("row", "col"),
        P("row", "col"),
        P("row", "col"),
        P("row", "col"),
        P("row", "col"),
    )
    out_specs = (P("row", "col"), P("row", "col"), P("row", "col"))
    return jax.shard_map(
        per_device, mesh=mesh, in_specs=in_specs, out_specs=out_specs, check_vma=False
    )
```

```python
import functools

import jax
import jax.numpy as jnp
from jax import lax
from jax.experimental import pallas as pl
from jax.experimental.pallas import tpu as pltpu
from jax.sharding import PartitionSpec as P

MESH = pl.DeviceIdType.MESH
NG = 8
HEAD = (
    ("a", 0), ("o", 0), ("o", 1), ("a", 1), ("a", 2), ("a", 3),
    ("a", 4), ("a", 5), ("a", 6), ("a", 7), ("b", 0), ("b", 1),
    ("b", 2), ("b", 3), ("z0", 1), ("z1", 1), ("z0", 2), ("c", 0),
    ("b", 4), ("c", 1), ("b", 5), ("c", 2), ("b", 6), ("c", 3),
    ("b", 7), ("z1", 2), ("z0", 3), ("d", 0), ("c", 4), ("d", 1),
    ("c", 5), ("d", 2), ("c", 6), ("z1", 3), ("d", 3), ("c", 7),
    ("l", 0), ("s", 0), ("e", 0), ("d", 4), ("l", 1), ("e", 1),
    ("d", 5), ("e", 2), ("d", 6), ("s", 1),
)
TAIL = (
    (),
    (("e", 3), ("d", 7),),
    (),
    (("e", 4),),
    (("e", 5),),
    (("e", 6),),
    (("e", 7),),
    (),
)

def split(v):
    hi = v.astype(jnp.bfloat16)
    return hi, (v - hi.astype(jnp.float32)).astype(jnp.bfloat16)


def dot3(a, b):
    f = functools.partial(jnp.dot, preferred_element_type=jnp.float32)
    return f(a[0], b[0]) + (f(a[0], b[1]) + f(a[1], b[0]))


def panel_product(grid, st, g):
    acc = None
    for p in range(2):
        m = split(grid[g, p].reshape(32 * 16, grid.shape[-1]))
        t = dot3((st[p, 0], st[p, 1]), m)
        acc = t if acc is None else acc + t
    return acc


def finish(out1, out2, upd, grid, st, o1, o2, o3, tail, sem):
    rows = grid.shape[-1]
    done = (NG - 1) * rows
    copies = [
        pltpu.make_async_copy(upd.at[pl.ds(0, done)], o3.at[pl.ds(0, done)], sem.at[0]),
        pltpu.make_async_copy(out1, o1, sem.at[1]),
        pltpu.make_async_copy(out2, o2, sem.at[2]),
    ]
    for c in copies:
        c.start()
    tail[...] = upd[pl.ds(done, rows), :] - panel_product(grid, st, NG - 1).T
    last = pltpu.make_async_copy(tail, o3.at[pl.ds(done, rows)], sem.at[3])
    last.start()
    for c in copies:
        c.wait()
    last.wait()


def kernel(
    a1, a2, cp, pt0, pt1, r1, r2, rest,
    out1, out2, upd, grid, st,
    zb1, zb2, xb1, xb2, sol,
    rsem, ssem, lsem, zrsem, zssem, zlsem, bsem,
):
    rows = pt0.shape[1] // NG
    z = lax.axis_index("row")
    col = lax.axis_index("col")
    y, x, h = col // 8, (col // 2) % 4, col % 2
    oh = 1 - h

    def cid(yy, xx, hh):
        return (yy * 4 + xx) * 2 + hh

    xp = (z, cid(y, (x + 1) % 4, h))
    xm = (z, cid(y, (x + 3) % 4, h))
    yp = (z, cid((y + 1) % 4, x, h))
    ym = (z, cid((y + 3) % 4, x, h))
    zp = ((z + 1) % 8, col)
    zm = ((z + 7) % 8, col)
    sib = (z, cid(y, x, oh))

    def send(src, dst, s, r, dev):
        pltpu.make_async_remote_copy(
            src_ref=src, dst_ref=dst, send_sem=s, recv_sem=r,
            device_id=dev, device_id_type=MESH,
        ).start()

    def take(ref, sem):
        pltpu.make_async_copy(ref, ref, sem).wait()

    panels = (
        (pt0, x, y, xp, xm, yp, ym),
        (pt1, y, x, yp, ym, xp, xm),
    )

    def local_own(g, p):
        pt, a, b = panels[p][:3]
        src = pt.at[:, pl.ds(pl.multiple_of(g * rows, rows), rows)]
        return pltpu.make_async_copy(src, grid.at[g, p, h, b, a], lsem.at[g, p])

    def stage_a(g):
        for p in range(2):
            pt, a, b, ap, am, bp, bm = panels[p]
            src = pt.at[:, pl.ds(pl.multiple_of(g * rows, rows), rows)]
            dst = grid.at[g, p, h, b, a]
            s = ssem.at[g, p]
            send(src, dst, s, rsem.at[g, p, 0], ap)
            send(src, dst, s, rsem.at[g, p, 1], am)
            send(src, dst, s, rsem.at[g, p, 3], bp)
            send(src, dst, s, rsem.at[g, p, 4], bm)

    def stage_b(g):
        for p in range(2):
            pt, a, b, ap, am, bp, bm = panels[p]
            s = ssem.at[g, p]
            for k, da, to, half in ((0, 3, ap, 0), (1, 1, am, 8)):
                ai = (a + da) % 4
                ref = grid.at[g, p, h, b, ai]
                take(ref, rsem.at[g, p, k])
                part = grid.at[g, p, h, b, ai, pl.ds(half, 8)]
                send(part, part, s, rsem.at[g, p, 2], to)
                send(ref, ref, s, rsem.at[g, p, 3], bp)
                send(ref, ref, s, rsem.at[g, p, 4], bm)

    def stage_c(g):
        for p in range(2):
            pt, a, b, ap, am, bp, bm = panels[p]
            s = ssem.at[g, p]
            ref = grid.at[g, p, h, b, (a + 2) % 4]
            take(ref, rsem.at[g, p, 2])
            send(ref, ref, s, rsem.at[g, p, 3], bp)
            send(ref, ref, s, rsem.at[g, p, 4], bm)
            local_own(g, p).wait()
            ref = grid.at[g, p, h, b]
            send(ref, ref, bsem.at[g, p], rsem.at[g, p, 6], sib)

    def stage_d(g):
        for p in range(2):
            pt, a, b, ap, am, bp, bm = panels[p]
            s = ssem.at[g, p]
            for k, db, to, half in ((3, 3, bp, 0), (4, 1, bm, 2)):
                bi = (b + db) % 4
                ref = grid.at[g, p, h, bi]
                take(ref, rsem.at[g, p, k])
                part = grid.at[g, p, h, bi, pl.ds(half, 2)]
                send(part, part, s, rsem.at[g, p, 5], to)
                send(ref, ref, bsem.at[g, p], rsem.at[g, p, 6], sib)

    def stage_e(g):
        for p in range(2):
            b = panels[p][2]
            ref = grid.at[g, p, h, (b + 2) % 4]
            take(ref, rsem.at[g, p, 5])
            send(ref, ref, bsem.at[g, p], rsem.at[g, p, 6], sib)

    def stage_f(g):
        for p in range(2):
            take(grid.at[g, p, oh], rsem.at[g, p, 6])
        here = pl.ds(pl.multiple_of(g * rows, rows), rows)
        upd[here, :] = upd[here, :] - panel_product(grid, st, g).T

    mcols = pl.ds(pl.multiple_of(h * 256, 256), 256)
    batches = (
        (zb1, (r1, a1.at[:, mcols])),
        (zb2, (r2, cp.at[:, mcols], a2.at[:, mcols])),
    )

    def z_own(bt):
        zb, items = batches[bt]
        for i, src in enumerate(items):
            dst = zb.at[z, i]
            send(src, dst, zssem.at[bt], zrsem.at[bt, 0], zp)
            send(src, dst, zssem.at[bt], zrsem.at[bt, 3], zm)

    def z_local(bt):
        zb, items = batches[bt]
        return [
            pltpu.make_async_copy(src, zb.at[z, i], zlsem.at[bt, i])
            for i, src in enumerate(items)
        ]

    def z_hop(bt, k):
        zb = batches[bt][0]
        for d, to, half, at in ((8 - k, zp, 0, 0), (k, zm, 32, 3)):
            zi = (z + d) % 8
            ref = zb.at[zi]
            take(ref, zrsem.at[bt, at + k - 1])
            if k < 3:
                send(ref, ref, zssem.at[bt], zrsem.at[bt, at + k], to)
            else:
                part = zb.at[zi, :, pl.ds(half, 32)]
                send(part, part, zssem.at[bt], zrsem.at[bt, 6], to)

    def z_last(bt):
        zb = batches[bt][0]
        take(zb.at[(z + 4) % 8], zrsem.at[bt, 6])
        for c in z_local(bt):
            c.wait()
        if bt == 0:
            send(zb1.at[:, pl.ds(1, 1)], xb1, zssem.at[2], zrsem.at[0, 7], sib)
        else:
            send(zb2.at[:, pl.ds(1, 2)], xb2, zssem.at[3], zrsem.at[1, 7], sib)

    def apply(own, other, load):
        here = split(load(h).reshape(256, 256))
        there = split(load(oh).reshape(256, 256))
        return dot3(split(own.reshape(512, 256)), here) + dot3(
            split(other.reshape(512, 256)), there
        )

    def keep(p, s):
        order = [
            (o // 4 % 4 * 4 + o % 4) * 2 + o // 16 if p == 0
            else (o % 4 * 4 + o // 4 % 4) * 2 + o // 16
            for o in range(32)
        ]
        perm = jnp.concatenate([s[c * 16:c * 16 + 16] for c in order], axis=0)
        hi, lo = split(perm.T)
        st[p, 0] = hi
        st[p, 1] = lo

    def solve_first():
        take(xb1, zrsem.at[0, 7])
        s = apply(
            zb1[:, 1], xb1[:, 0], lambda q: zb1[pl.ds(q * 4, 4), 0]
        )
        sol[0] = s.reshape(8, 64, 256)
        out1[...] = sol[0, z]
        keep(0, s)

    def solve_second():
        take(xb2, zrsem.at[1, 7])
        red = zb2[:, 0].reshape(512, 256) - apply(
            zb2[:, 1], xb2[:, 0], lambda q: sol[0, pl.ds(q * 4, 4)]
        )
        sol[1] = red.reshape(8, 64, 256)
        s = apply(
            zb2[:, 2], xb2[:, 1], lambda q: sol[1, pl.ds(q * 4, 4)]
        )
        sol[1] = s.reshape(8, 64, 256)
        out2[...] = sol[1, z]
        keep(1, s)

    barrier = pltpu.get_barrier_semaphore()
    near = (xp, xm, yp, ym, zp, zm, sib)
    for dev in near:
        pl.semaphore_signal(barrier, inc=1, device_id=dev, device_id_type=MESH)
    pl.semaphore_wait(barrier, len(near))

    stages = {
        "a": stage_a,
        "b": stage_b,
        "c": stage_c,
        "d": stage_d,
        "e": stage_e,
        "o": z_own,
        "l": z_last,
        "s": lambda bt: (solve_first, solve_second)[bt](),
        "z0": lambda k: z_hop(0, k),
        "z1": lambda k: z_hop(1, k),
    }

    def run(steps):
        for name, arg in steps:
            stages[name](arg)

    def local_starts():
        @pl.loop(0, NG)
        def _(g):
            for p in range(2):
                local_own(g, p).start()

        for bt in range(2):
            for c in z_local(bt):
                c.start()
        rest_copy.start()

    rest_copy = pltpu.make_async_copy(rest, upd, zlsem.at[0, 2])
    count = sum(name in ("a", "o") for name, _ in HEAD)
    run(HEAD[:count])
    local_starts()
    run(HEAD[count:])
    rest_copy.wait()

    @pl.loop(0, NG - 1)
    def _(g):
        for k in range(NG - 1):
            if TAIL[k]:
                @pl.when(g == k)
                def _(k=k):
                    run(TAIL[k])

        stage_f(g)

    run(TAIL[NG - 1])

    for p in range(2):
        take(grid.at[NG - 1, p, oh], rsem.at[NG - 1, p, 6])

    @pl.loop(0, NG)
    def _(g):
        for p in range(2):
            take(upd.at[pl.ds(0, 15 * rows // 16)], ssem.at[g, p])
            take(grid.at[g, p, h], bsem.at[g, p])

    take(zb1.at[pl.ds(0, 7)], zssem.at[0])
    take(zb2.at[pl.ds(0, 7)], zssem.at[1])
    take(xb1, zssem.at[2])
    take(xb2, zssem.at[3])


def per_device(
    inverse_first,
    inverse_second,
    coupling,
    panel_first,
    panel_second,
    rhs_first,
    rhs_second,
    rhs_rest,
):
    rows = rhs_rest.shape[0]
    f32 = jnp.float32
    group = rows // NG
    any_spec = pl.BlockSpec(memory_space=pltpu.HBM)
    vmem_spec = pl.BlockSpec(memory_space=pltpu.VMEM)
    sem = pltpu.SemaphoreType.DMA
    mid = pl.pallas_call(
        kernel,
        out_shape=(
            pltpu.VMEM((64, 256), f32),
            pltpu.VMEM((64, 256), f32),
            pltpu.VMEM((rows, 256), f32),
            pltpu.VMEM((NG, 2, 2, 4, 4, 16, group), f32),
            pltpu.VMEM((2, 2, 256, 512), jnp.bfloat16),
        ),
        in_specs=[any_spec] * 8,
        out_specs=(vmem_spec,) * 5,
        scratch_shapes=[
            pltpu.VMEM((8, 2, 64, 256), f32),
            pltpu.VMEM((8, 3, 64, 256), f32),
            pltpu.VMEM((8, 1, 64, 256), f32),
            pltpu.VMEM((8, 2, 64, 256), f32),
            pltpu.VMEM((2, 8, 64, 256), f32),
            sem((NG, 2, 7)),
            sem((NG, 2)),
            sem((NG, 2)),
            sem((2, 8)),
            sem((4,)),
            sem((2, 3)),
            sem((NG, 2)),
        ],
        compiler_params=pltpu.CompilerParams(
            collective_id=0, has_side_effects=True, vmem_limit_bytes=24 * 1024 * 1024
        ),
    )(
        *(
            pltpu.with_memory_space_constraint(v, pltpu.HBM)
            for v in (
                inverse_first,
                inverse_second,
                coupling,
                panel_first.T,
                panel_second.T,
                rhs_first,
                rhs_second,
                rhs_rest,
            )
        )
    )
    return pl.pallas_call(
        finish,
        out_shape=(
            jax.ShapeDtypeStruct((64, 256), f32),
            jax.ShapeDtypeStruct((64, 256), f32),
            jax.ShapeDtypeStruct((rows, 256), f32),
        ),
        in_specs=[vmem_spec] * 5,
        out_specs=(any_spec,) * 3,
        scratch_shapes=[pltpu.VMEM((group, 256), f32), sem((4,))],
        compiler_params=pltpu.CompilerParams(vmem_limit_bytes=16 * 1024 * 1024),
    )(*mid)


def solution(mesh):
    in_specs = (
        P("row", None),
        P("row", None),
        P("row", None),
        P("row", "col"),
        P("row", "col"),
        P("row", "col"),
        P("row", "col"),
        P("row", "col"),
    )
    out_specs = (P("row", "col"), P("row", "col"), P("row", "col"))
    return jax.shard_map(
        per_device, mesh=mesh, in_specs=in_specs, out_specs=out_specs, check_vma=False
    )
```

```python
import functools

import jax
import jax.numpy as jnp
from jax import lax
from jax.experimental import pallas as pl
from jax.experimental.pallas import tpu as pltpu
from jax.sharding import PartitionSpec as P

MESH = pl.DeviceIdType.MESH
NG = 8
HEAD = (
    ("a", 0), ("a", 1), ("o", 0), ("a", 2), ("a", 3), ("o", 1),
    ("a", 4), ("b", 0), ("a", 5), ("b", 1), ("b", 2), ("a", 6),
    ("z0", 1), ("z1", 1), ("a", 7), ("c", 0), ("b", 3), ("b", 4),
    ("c", 1), ("z0", 2), ("c", 2), ("b", 5), ("z1", 2), ("b", 6),
    ("b", 7), ("z0", 3), ("c", 3), ("d", 0), ("c", 4), ("d", 1),
    ("z1", 3), ("c", 5), ("c", 6), ("d", 2), ("l", 0), ("c", 7),
    ("d", 3), ("l", 1), ("d", 4), ("e", 0), ("d", 5), ("s", 0),
    ("e", 1), ("s", 1), ("d", 6),
)
TAIL = (
    (),
    (("e", 2), ("d", 7),),
    (("e", 3),),
    (("e", 4),),
    (("e", 5),),
    (("e", 6),),
    (("e", 7),),
    (),
)

def split(v):
    hi = v.astype(jnp.bfloat16)
    return hi, (v - hi.astype(jnp.float32)).astype(jnp.bfloat16)


def dot3(a, b):
    f = functools.partial(jnp.dot, preferred_element_type=jnp.float32)
    return f(a[0], b[0]) + (f(a[0], b[1]) + f(a[1], b[0]))


def panel_product(grid, st, g):
    acc = None
    for p in range(2):
        m = split(grid[g, p].reshape(32 * 16, grid.shape[-1]))
        t = dot3((st[p, 0], st[p, 1]), m)
        acc = t if acc is None else acc + t
    return acc


def finish(out1, out2, upd, grid, st, o1, o2, o3, tail, sem):
    rows = grid.shape[-1]
    done = (NG - 1) * rows
    copies = [
        pltpu.make_async_copy(upd.at[pl.ds(0, done)], o3.at[pl.ds(0, done)], sem.at[0]),
        pltpu.make_async_copy(out1, o1, sem.at[1]),
        pltpu.make_async_copy(out2, o2, sem.at[2]),
    ]
    for c in copies:
        c.start()
    tail[...] = upd[pl.ds(done, rows), :] - panel_product(grid, st, NG - 1).T
    last = pltpu.make_async_copy(tail, o3.at[pl.ds(done, rows)], sem.at[3])
    last.start()
    for c in copies:
        c.wait()
    last.wait()


def kernel(
    a1, a2, cp, pt0, pt1, r1, r2, rest,
    out1, out2, upd, grid, st,
    zb1, zb2, xb1, xb2, sol,
    rsem, ssem, lsem, zrsem, zssem, zlsem, bsem, ready,
):
    rows = pt0.shape[1] // NG
    z = lax.axis_index("row")
    col = lax.axis_index("col")
    y, x, h = col // 8, (col // 2) % 4, col % 2
    oh = 1 - h

    def cid(yy, xx, hh):
        return (yy * 4 + xx) * 2 + hh

    xp = (z, cid(y, (x + 1) % 4, h))
    xm = (z, cid(y, (x + 3) % 4, h))
    yp = (z, cid((y + 1) % 4, x, h))
    ym = (z, cid((y + 3) % 4, x, h))
    zp = ((z + 1) % 8, col)
    zm = ((z + 7) % 8, col)
    sib = (z, cid(y, x, oh))

    def send(src, dst, s, r, dev):
        pltpu.make_async_remote_copy(
            src_ref=src, dst_ref=dst, send_sem=s, recv_sem=r,
            device_id=dev, device_id_type=MESH,
        ).start()

    def take(ref, sem):
        pltpu.make_async_copy(ref, ref, sem).wait()

    panels = (
        (pt0, x, y, xp, xm, yp, ym),
        (pt1, y, x, yp, ym, xp, xm),
    )

    def local_own(g, p):
        pt, a, b = panels[p][:3]
        src = pt.at[:, pl.ds(pl.multiple_of(g * rows, rows), rows)]
        return pltpu.make_async_copy(src, grid.at[g, p, h, b, a], lsem.at[g, p])

    def stage_a(g):
        for p in range(2):
            pt, a, b, ap, am, bp, bm = panels[p]
            src = pt.at[:, pl.ds(pl.multiple_of(g * rows, rows), rows)]
            dst = grid.at[g, p, h, b, a]
            s = ssem.at[g, p]
            send(src, dst, s, rsem.at[g, p, 0], ap)
            send(src, dst, s, rsem.at[g, p, 1], am)
            send(src, dst, s, rsem.at[g, p, 3], bp)
            send(src, dst, s, rsem.at[g, p, 4], bm)

    def stage_b(g):
        for p in range(2):
            pt, a, b, ap, am, bp, bm = panels[p]
            s = ssem.at[g, p]
            for k, da, to, half in ((0, 3, ap, 0), (1, 1, am, 8)):
                ai = (a + da) % 4
                ref = grid.at[g, p, h, b, ai]
                take(ref, rsem.at[g, p, k])
                part = grid.at[g, p, h, b, ai, pl.ds(half, 8)]
                send(part, part, s, rsem.at[g, p, 2], to)
                send(ref, ref, s, rsem.at[g, p, 3], bp)
                send(ref, ref, s, rsem.at[g, p, 4], bm)

    def stage_c(g):
        for p in range(2):
            pt, a, b, ap, am, bp, bm = panels[p]
            s = ssem.at[g, p]
            ref = grid.at[g, p, h, b, (a + 2) % 4]
            take(ref, rsem.at[g, p, 2])
            send(ref, ref, s, rsem.at[g, p, 3], bp)
            send(ref, ref, s, rsem.at[g, p, 4], bm)
            local_own(g, p).wait()
            ref = grid.at[g, p, h, b]
            send(ref, ref, bsem.at[g, p], rsem.at[g, p, 6], sib)

    def stage_d(g):
        for p in range(2):
            pt, a, b, ap, am, bp, bm = panels[p]
            s = ssem.at[g, p]
            for k, db, to, half in ((3, 3, bp, 0), (4, 1, bm, 2)):
                bi = (b + db) % 4
                ref = grid.at[g, p, h, bi]
                take(ref, rsem.at[g, p, k])
                part = grid.at[g, p, h, bi, pl.ds(half, 2)]
                send(part, part, s, rsem.at[g, p, 5], to)
                send(ref, ref, bsem.at[g, p], rsem.at[g, p, 6], sib)

    def stage_e(g):
        for p in range(2):
            b = panels[p][2]
            ref = grid.at[g, p, h, (b + 2) % 4]
            take(ref, rsem.at[g, p, 5])
            send(ref, ref, bsem.at[g, p], rsem.at[g, p, 6], sib)

    def stage_f(g):
        for p in range(2):
            take(grid.at[g, p, oh], rsem.at[g, p, 6])
        here = pl.ds(pl.multiple_of(g * rows, rows), rows)
        upd[here, :] = upd[here, :] - panel_product(grid, st, g).T

    mcols = pl.ds(pl.multiple_of(h * 256, 256), 256)
    batches = (
        (zb1, (r1, a1.at[:, mcols])),
        (zb2, (r2, cp.at[:, mcols], a2.at[:, mcols])),
    )

    def z_own(bt):
        zb, items = batches[bt]
        for i, src in enumerate(items):
            dst = zb.at[z, i]
            send(src, dst, zssem.at[bt], zrsem.at[bt, 0], zp)
            send(src, dst, zssem.at[bt], zrsem.at[bt, 3], zm)

    def z_local(bt):
        zb, items = batches[bt]
        return [
            pltpu.make_async_copy(src, zb.at[z, i], zlsem.at[bt, i])
            for i, src in enumerate(items)
        ]

    def z_hop(bt, k):
        zb = batches[bt][0]
        for d, to, half, at in ((8 - k, zp, 0, 0), (k, zm, 32, 3)):
            zi = (z + d) % 8
            ref = zb.at[zi]
            take(ref, zrsem.at[bt, at + k - 1])
            if k < 3:
                send(ref, ref, zssem.at[bt], zrsem.at[bt, at + k], to)
            else:
                part = zb.at[zi, :, pl.ds(half, 32)]
                send(part, part, zssem.at[bt], zrsem.at[bt, 6], to)

    def z_last(bt):
        zb = batches[bt][0]
        take(zb.at[(z + 4) % 8], zrsem.at[bt, 6])
        for c in z_local(bt):
            c.wait()
        if bt == 0:
            send(zb1.at[:, pl.ds(1, 1)], xb1, zssem.at[2], zrsem.at[0, 7], sib)
        else:
            send(zb2.at[:, pl.ds(1, 2)], xb2, zssem.at[3], zrsem.at[1, 7], sib)

    def apply(own, other, load):
        here = split(load(h).reshape(256, 256))
        there = split(load(oh).reshape(256, 256))
        return dot3(split(own.reshape(512, 256)), here) + dot3(
            split(other.reshape(512, 256)), there
        )

    def keep(p, s):
        order = [
            (o // 4 % 4 * 4 + o % 4) * 2 + o // 16 if p == 0
            else (o % 4 * 4 + o // 4 % 4) * 2 + o // 16
            for o in range(32)
        ]
        perm = jnp.concatenate([s[c * 16:c * 16 + 16] for c in order], axis=0)
        hi, lo = split(perm.T)
        st[p, 0] = hi
        st[p, 1] = lo

    def solve_first():
        take(xb1, zrsem.at[0, 7])
        s = apply(
            zb1[:, 1], xb1[:, 0], lambda q: zb1[pl.ds(q * 4, 4), 0]
        )
        sol[0] = s.reshape(8, 64, 256)
        out1[...] = sol[0, z]
        keep(0, s)

    def solve_second():
        take(xb2, zrsem.at[1, 7])
        red = zb2[:, 0].reshape(512, 256) - apply(
            zb2[:, 1], xb2[:, 0], lambda q: sol[0, pl.ds(q * 4, 4)]
        )
        sol[1] = red.reshape(8, 64, 256)
        s = apply(
            zb2[:, 2], xb2[:, 1], lambda q: sol[1, pl.ds(q * 4, 4)]
        )
        sol[1] = s.reshape(8, 64, 256)
        out2[...] = sol[1, z]
        keep(1, s)

    def tell(sem, dev):
        pl.semaphore_signal(sem, inc=1, device_id=dev, device_id_type=MESH)

    barrier = pltpu.get_barrier_semaphore()
    for yy, xx in ((y, x + 1), (y, x + 3), (y + 1, x), (y + 3, x)):
        tell(barrier, (z, cid(yy % 4, xx % 4, 0)))
    for zz in (z + 1, z + 7):
        tell(barrier, (zz % 8, cid(y, x, 1)))

    @pl.when(h == 1)
    def _():
        tell(barrier, sib)

    @pl.when(h == 0)
    def _():
        pl.semaphore_wait(barrier, 9)
        tell(ready, sib)

    @pl.when(h == 1)
    def _():
        pl.semaphore_wait(ready, 1)

    def z_ready():
        @pl.when(h == 1)
        def _():
            pl.semaphore_wait(barrier, 4)
            tell(ready, sib)

        @pl.when(h == 0)
        def _():
            pl.semaphore_wait(ready, 1)

    def z_first(bt):
        if bt == 0:
            z_ready()
        z_own(bt)

    stages = {
        "a": stage_a,
        "b": stage_b,
        "c": stage_c,
        "d": stage_d,
        "e": stage_e,
        "o": z_first,
        "l": z_last,
        "s": lambda bt: (solve_first, solve_second)[bt](),
        "z0": lambda k: z_hop(0, k),
        "z1": lambda k: z_hop(1, k),
    }

    def run(steps):
        for name, arg in steps:
            stages[name](arg)

    def local_starts():
        @pl.loop(0, NG)
        def _(g):
            for p in range(2):
                local_own(g, p).start()

        for bt in range(2):
            for c in z_local(bt):
                c.start()
        rest_copy.start()

    rest_copy = pltpu.make_async_copy(rest, upd, zlsem.at[0, 2])
    run(HEAD[:3])
    local_starts()
    run(HEAD[3:])
    rest_copy.wait()

    @pl.loop(0, NG - 1)
    def _(g):
        for k in range(NG - 1):
            if TAIL[k]:
                @pl.when(g == k)
                def _(k=k):
                    run(TAIL[k])

        stage_f(g)

    run(TAIL[NG - 1])

    for p in range(2):
        take(grid.at[NG - 1, p, oh], rsem.at[NG - 1, p, 6])

    @pl.loop(0, NG)
    def _(g):
        for p in range(2):
            take(upd.at[pl.ds(0, 15 * rows // 16)], ssem.at[g, p])
            take(grid.at[g, p, h], bsem.at[g, p])

    take(zb1.at[pl.ds(0, 7)], zssem.at[0])
    take(zb2.at[pl.ds(0, 7)], zssem.at[1])
    take(xb1, zssem.at[2])
    take(xb2, zssem.at[3])


def per_device(
    inverse_first,
    inverse_second,
    coupling,
    panel_first,
    panel_second,
    rhs_first,
    rhs_second,
    rhs_rest,
):
    rows = rhs_rest.shape[0]
    f32 = jnp.float32
    group = rows // NG
    any_spec = pl.BlockSpec(memory_space=pltpu.HBM)
    vmem_spec = pl.BlockSpec(memory_space=pltpu.VMEM)
    sem = pltpu.SemaphoreType.DMA
    mid = pl.pallas_call(
        kernel,
        out_shape=(
            pltpu.VMEM((64, 256), f32),
            pltpu.VMEM((64, 256), f32),
            pltpu.VMEM((rows, 256), f32),
            pltpu.VMEM((NG, 2, 2, 4, 4, 16, group), f32),
            pltpu.VMEM((2, 2, 256, 512), jnp.bfloat16),
        ),
        in_specs=[any_spec] * 8,
        out_specs=(vmem_spec,) * 5,
        scratch_shapes=[
            pltpu.VMEM((8, 2, 64, 256), f32),
            pltpu.VMEM((8, 3, 64, 256), f32),
            pltpu.VMEM((8, 1, 64, 256), f32),
            pltpu.VMEM((8, 2, 64, 256), f32),
            pltpu.VMEM((2, 8, 64, 256), f32),
            sem((NG, 2, 7)),
            sem((NG, 2)),
            sem((NG, 2)),
            sem((2, 8)),
            sem((4,)),
            sem((2, 3)),
            sem((NG, 2)),
            pltpu.SemaphoreType.REGULAR,
        ],
        compiler_params=pltpu.CompilerParams(
            collective_id=0, has_side_effects=True, vmem_limit_bytes=24 * 1024 * 1024
        ),
    )(
        *(
            pltpu.with_memory_space_constraint(v, pltpu.HBM)
            for v in (
                inverse_first,
                inverse_second,
                coupling,
                panel_first.T,
                panel_second.T,
                rhs_first,
                rhs_second,
                rhs_rest,
            )
        )
    )
    return pl.pallas_call(
        finish,
        out_shape=(
            jax.ShapeDtypeStruct((64, 256), f32),
            jax.ShapeDtypeStruct((64, 256), f32),
            jax.ShapeDtypeStruct((rows, 256), f32),
        ),
        in_specs=[vmem_spec] * 5,
        out_specs=(any_spec,) * 3,
        scratch_shapes=[pltpu.VMEM((group, 256), f32), sem((4,))],
        compiler_params=pltpu.CompilerParams(vmem_limit_bytes=16 * 1024 * 1024),
    )(*mid)


def solution(mesh):
    in_specs = (
        P("row", None),
        P("row", None),
        P("row", None),
        P("row", "col"),
        P("row", "col"),
        P("row", "col"),
        P("row", "col"),
        P("row", "col"),
    )
    out_specs = (P("row", "col"), P("row", "col"), P("row", "col"))
    return jax.shard_map(
        per_device, mesh=mesh, in_specs=in_specs, out_specs=out_specs, check_vma=False
    )
```

```python
import functools

import jax
import jax.numpy as jnp
from jax import lax
from jax.experimental import pallas as pl
from jax.experimental.pallas import tpu as pltpu
from jax.sharding import PartitionSpec as P

MESH = pl.DeviceIdType.MESH
NG = 8
HEAD = (
    ("a", 0), ("a", 1), ("a", 2), ("a", 3), ("a", 4), ("a", 5),
    ("o", 0), ("o", 1), ("b", 0), ("b", 1), ("a", 6), ("z0", 1),
    ("b", 2), ("z1", 1), ("b", 3), ("b", 4), ("z0", 2), ("c", 0),
    ("a", 7), ("c", 1), ("b", 5), ("b", 6), ("z1", 2), ("c", 2),
    ("z0", 3), ("b", 7), ("c", 3), ("c", 4), ("d", 0), ("d", 1),
    ("z1", 3), ("c", 5), ("c", 6), ("d", 2), ("c", 7), ("l", 0),
    ("d", 3), ("d", 4), ("l", 1), ("s", 0), ("e", 0), ("e", 1),
    ("d", 5), ("d", 6), ("s", 1), ("e", 2),
)
TAIL = (
    (),
    (("d", 7),),
    (("e", 3),),
    (("e", 4),),
    (("e", 5),),
    (("e", 6),),
    (("e", 7),),
    (),
)

def split(v):
    hi = v.astype(jnp.bfloat16)
    return hi, (v - hi.astype(jnp.float32)).astype(jnp.bfloat16)


def dot3(a, b):
    f = functools.partial(jnp.dot, preferred_element_type=jnp.float32)
    return f(a[0], b[0]) + (f(a[0], b[1]) + f(a[1], b[0]))


def panel_product(grid, st, g):
    acc = None
    for p in range(2):
        m = split(grid[g, p].reshape(32 * 16, grid.shape[-1]))
        t = dot3((st[p, 0], st[p, 1]), m)
        acc = t if acc is None else acc + t
    return acc


def finish(out1, out2, upd, grid, st, o1, o2, o3, tail, sem):
    rows = grid.shape[-1]
    done = (NG - 1) * rows
    copies = [
        pltpu.make_async_copy(upd.at[pl.ds(0, done)], o3.at[pl.ds(0, done)], sem.at[0]),
        pltpu.make_async_copy(out1, o1, sem.at[1]),
        pltpu.make_async_copy(out2, o2, sem.at[2]),
    ]
    for c in copies:
        c.start()
    tail[...] = upd[pl.ds(done, rows), :] - panel_product(grid, st, NG - 1).T
    last = pltpu.make_async_copy(tail, o3.at[pl.ds(done, rows)], sem.at[3])
    last.start()
    for c in copies:
        c.wait()
    last.wait()


def kernel(
    a1, a2, cp, pt0, pt1, r1, r2, rest,
    out1, out2, upd, grid, st,
    zb1, zb2, xb1, xb2, sol,
    rsem, ssem, lsem, zrsem, zssem, zlsem, bsem, ready,
):
    rows = pt0.shape[1] // NG
    z = lax.axis_index("row")
    col = lax.axis_index("col")
    y, x, h = col // 8, (col // 2) % 4, col % 2
    oh = 1 - h

    def cid(yy, xx, hh):
        return (yy * 4 + xx) * 2 + hh

    xp = (z, cid(y, (x + 1) % 4, h))
    xm = (z, cid(y, (x + 3) % 4, h))
    yp = (z, cid((y + 1) % 4, x, h))
    ym = (z, cid((y + 3) % 4, x, h))
    zp = ((z + 1) % 8, col)
    zm = ((z + 7) % 8, col)
    sib = (z, cid(y, x, oh))

    def send(src, dst, s, r, dev):
        pltpu.make_async_remote_copy(
            src_ref=src, dst_ref=dst, send_sem=s, recv_sem=r,
            device_id=dev, device_id_type=MESH,
        ).start()

    def take(ref, sem):
        pltpu.make_async_copy(ref, ref, sem).wait()

    panels = (
        (pt0, x, y, xp, xm, yp, ym),
        (pt1, y, x, yp, ym, xp, xm),
    )

    def local_own(g, p):
        pt, a, b = panels[p][:3]
        src = pt.at[:, pl.ds(pl.multiple_of(g * rows, rows), rows)]
        return pltpu.make_async_copy(src, grid.at[g, p, h, b, a], lsem.at[g, p])

    def stage_a(g):
        for p in range(2):
            pt, a, b, ap, am, bp, bm = panels[p]
            src = pt.at[:, pl.ds(pl.multiple_of(g * rows, rows), rows)]
            dst = grid.at[g, p, h, b, a]
            s = ssem.at[g, p]
            send(src, dst, s, rsem.at[g, p, 0], ap)
            send(src, dst, s, rsem.at[g, p, 1], am)
            send(src, dst, s, rsem.at[g, p, 3], bp)
            send(src, dst, s, rsem.at[g, p, 4], bm)

    def stage_b(g):
        for p in range(2):
            pt, a, b, ap, am, bp, bm = panels[p]
            s = ssem.at[g, p]
            for k, da, to, half in ((0, 3, ap, 0), (1, 1, am, 8)):
                ai = (a + da) % 4
                ref = grid.at[g, p, h, b, ai]
                take(ref, rsem.at[g, p, k])
                part = grid.at[g, p, h, b, ai, pl.ds(half, 8)]
                send(part, part, s, rsem.at[g, p, 2], to)
                send(ref, ref, s, rsem.at[g, p, 3], bp)
                send(ref, ref, s, rsem.at[g, p, 4], bm)

    def stage_c(g):
        for p in range(2):
            pt, a, b, ap, am, bp, bm = panels[p]
            s = ssem.at[g, p]
            ref = grid.at[g, p, h, b, (a + 2) % 4]
            take(ref, rsem.at[g, p, 2])
            send(ref, ref, s, rsem.at[g, p, 3], bp)
            send(ref, ref, s, rsem.at[g, p, 4], bm)
            local_own(g, p).wait()
            ref = grid.at[g, p, h, b]
            send(ref, ref, bsem.at[g, p], rsem.at[g, p, 6], sib)

    def stage_d(g):
        for p in range(2):
            pt, a, b, ap, am, bp, bm = panels[p]
            s = ssem.at[g, p]
            for k, db, to, half in ((3, 3, bp, 0), (4, 1, bm, 2)):
                bi = (b + db) % 4
                ref = grid.at[g, p, h, bi]
                take(ref, rsem.at[g, p, k])
                part = grid.at[g, p, h, bi, pl.ds(half, 2)]
                send(part, part, s, rsem.at[g, p, 5], to)
                send(ref, ref, bsem.at[g, p], rsem.at[g, p, 6], sib)

    def stage_e(g):
        for p in range(2):
            b = panels[p][2]
            ref = grid.at[g, p, h, (b + 2) % 4]
            take(ref, rsem.at[g, p, 5])
            send(ref, ref, bsem.at[g, p], rsem.at[g, p, 6], sib)

    def stage_f(g):
        for p in range(2):
            take(grid.at[g, p, oh], rsem.at[g, p, 6])
        here = pl.ds(pl.multiple_of(g * rows, rows), rows)
        upd[here, :] = upd[here, :] - panel_product(grid, st, g).T

    mcols = pl.ds(pl.multiple_of(h * 256, 256), 256)
    batches = (
        (zb1, (r1, a1.at[:, mcols])),
        (zb2, (r2, cp.at[:, mcols], a2.at[:, mcols])),
    )

    def z_own(bt):
        zb, items = batches[bt]
        for i, src in enumerate(items):
            dst = zb.at[z, i]
            send(src, dst, zssem.at[bt], zrsem.at[bt, 0], zp)
            send(src, dst, zssem.at[bt], zrsem.at[bt, 3], zm)

    def z_local(bt):
        zb, items = batches[bt]
        return [
            pltpu.make_async_copy(src, zb.at[z, i], zlsem.at[bt, i])
            for i, src in enumerate(items)
        ]

    def z_hop(bt, k):
        zb = batches[bt][0]
        for d, to, half, at in ((8 - k, zp, 0, 0), (k, zm, 32, 3)):
            zi = (z + d) % 8
            ref = zb.at[zi]
            take(ref, zrsem.at[bt, at + k - 1])
            if k < 3:
                send(ref, ref, zssem.at[bt], zrsem.at[bt, at + k], to)
            else:
                part = zb.at[zi, :, pl.ds(half, 32)]
                send(part, part, zssem.at[bt], zrsem.at[bt, 6], to)

    def z_last(bt):
        zb = batches[bt][0]
        take(zb.at[(z + 4) % 8], zrsem.at[bt, 6])
        for c in z_local(bt):
            c.wait()
        if bt == 0:
            send(zb1.at[:, pl.ds(1, 1)], xb1, zssem.at[2], zrsem.at[0, 7], sib)
        else:
            send(zb2.at[:, pl.ds(1, 2)], xb2, zssem.at[3], zrsem.at[1, 7], sib)

    def apply(own, other, load):
        here = split(load(h).reshape(256, 256))
        there = split(load(oh).reshape(256, 256))
        return dot3(split(own.reshape(512, 256)), here) + dot3(
            split(other.reshape(512, 256)), there
        )

    def keep(p, s):
        order = [
            (o // 4 % 4 * 4 + o % 4) * 2 + o // 16 if p == 0
            else (o % 4 * 4 + o // 4 % 4) * 2 + o // 16
            for o in range(32)
        ]
        perm = jnp.concatenate([s[c * 16:c * 16 + 16] for c in order], axis=0)
        hi, lo = split(perm.T)
        st[p, 0] = hi
        st[p, 1] = lo

    def solve_first():
        take(xb1, zrsem.at[0, 7])
        s = apply(
            zb1[:, 1], xb1[:, 0], lambda q: zb1[pl.ds(q * 4, 4), 0]
        )
        sol[0] = s.reshape(8, 64, 256)
        out1[...] = sol[0, z]
        keep(0, s)

    def solve_second():
        take(xb2, zrsem.at[1, 7])
        red = zb2[:, 0].reshape(512, 256) - apply(
            zb2[:, 1], xb2[:, 0], lambda q: sol[0, pl.ds(q * 4, 4)]
        )
        sol[1] = red.reshape(8, 64, 256)
        s = apply(
            zb2[:, 2], xb2[:, 1], lambda q: sol[1, pl.ds(q * 4, 4)]
        )
        sol[1] = s.reshape(8, 64, 256)
        out2[...] = sol[1, z]
        keep(1, s)

    def tell(sem, dev):
        pl.semaphore_signal(sem, inc=1, device_id=dev, device_id_type=MESH)

    barrier = pltpu.get_barrier_semaphore()
    for yy, xx in ((y, x + 1), (y, x + 3), (y + 1, x), (y + 3, x)):
        tell(barrier, (z, cid(yy % 4, xx % 4, 0)))
    for zz in (z + 1, z + 7):
        tell(barrier, (zz % 8, cid(y, x, 1)))

    @pl.when(h == 1)
    def _():
        tell(barrier, sib)

    @pl.when(h == 0)
    def _():
        pl.semaphore_wait(barrier, 9)
        tell(ready, sib)

    @pl.when(h == 1)
    def _():
        pl.semaphore_wait(ready, 1)

    def z_ready():
        @pl.when(h == 1)
        def _():
            pl.semaphore_wait(barrier, 4)
            tell(ready, sib)

        @pl.when(h == 0)
        def _():
            pl.semaphore_wait(ready, 1)

    def z_first(bt):
        if bt == 0:
            z_ready()
        z_own(bt)

    stages = {
        "a": stage_a,
        "b": stage_b,
        "c": stage_c,
        "d": stage_d,
        "e": stage_e,
        "o": z_first,
        "l": z_last,
        "s": lambda bt: (solve_first, solve_second)[bt](),
        "z0": lambda k: z_hop(0, k),
        "z1": lambda k: z_hop(1, k),
    }

    def run(steps):
        for name, arg in steps:
            stages[name](arg)

    def local_starts():
        @pl.loop(0, NG)
        def _(g):
            for p in range(2):
                local_own(g, p).start()

        for bt in range(2):
            for c in z_local(bt):
                c.start()
        rest_copy.start()

    rest_copy = pltpu.make_async_copy(rest, upd, zlsem.at[0, 2])
    run(HEAD[:3])
    local_starts()
    run(HEAD[3:])
    rest_copy.wait()

    @pl.loop(0, NG - 1)
    def _(g):
        for k in range(NG - 1):
            if TAIL[k]:
                @pl.when(g == k)
                def _(k=k):
                    run(TAIL[k])

        stage_f(g)

    run(TAIL[NG - 1])

    for p in range(2):
        take(grid.at[NG - 1, p, oh], rsem.at[NG - 1, p, 6])

    @pl.loop(0, NG)
    def _(g):
        for p in range(2):
            take(upd.at[pl.ds(0, 15 * rows // 16)], ssem.at[g, p])
            take(grid.at[g, p, h], bsem.at[g, p])

    take(zb1.at[pl.ds(0, 7)], zssem.at[0])
    take(zb2.at[pl.ds(0, 7)], zssem.at[1])
    take(xb1, zssem.at[2])
    take(xb2, zssem.at[3])


def per_device(
    inverse_first,
    inverse_second,
    coupling,
    panel_first,
    panel_second,
    rhs_first,
    rhs_second,
    rhs_rest,
):
    rows = rhs_rest.shape[0]
    f32 = jnp.float32
    group = rows // NG
    any_spec = pl.BlockSpec(memory_space=pltpu.HBM)
    vmem_spec = pl.BlockSpec(memory_space=pltpu.VMEM)
    sem = pltpu.SemaphoreType.DMA
    mid = pl.pallas_call(
        kernel,
        out_shape=(
            pltpu.VMEM((64, 256), f32),
            pltpu.VMEM((64, 256), f32),
            pltpu.VMEM((rows, 256), f32),
            pltpu.VMEM((NG, 2, 2, 4, 4, 16, group), f32),
            pltpu.VMEM((2, 2, 256, 512), jnp.bfloat16),
        ),
        in_specs=[any_spec] * 8,
        out_specs=(vmem_spec,) * 5,
        scratch_shapes=[
            pltpu.VMEM((8, 2, 64, 256), f32),
            pltpu.VMEM((8, 3, 64, 256), f32),
            pltpu.VMEM((8, 1, 64, 256), f32),
            pltpu.VMEM((8, 2, 64, 256), f32),
            pltpu.VMEM((2, 8, 64, 256), f32),
            sem((NG, 2, 7)),
            sem((NG, 2)),
            sem((NG, 2)),
            sem((2, 8)),
            sem((4,)),
            sem((2, 3)),
            sem((NG, 2)),
            pltpu.SemaphoreType.REGULAR,
        ],
        compiler_params=pltpu.CompilerParams(
            collective_id=0, has_side_effects=True, vmem_limit_bytes=24 * 1024 * 1024
        ),
    )(
        *(
            pltpu.with_memory_space_constraint(v, pltpu.HBM)
            for v in (
                inverse_first,
                inverse_second,
                coupling,
                panel_first.T,
                panel_second.T,
                rhs_first,
                rhs_second,
                rhs_rest,
            )
        )
    )
    return pl.pallas_call(
        finish,
        out_shape=(
            jax.ShapeDtypeStruct((64, 256), f32),
            jax.ShapeDtypeStruct((64, 256), f32),
            jax.ShapeDtypeStruct((rows, 256), f32),
        ),
        in_specs=[vmem_spec] * 5,
        out_specs=(any_spec,) * 3,
        scratch_shapes=[pltpu.VMEM((group, 256), f32), sem((4,))],
        compiler_params=pltpu.CompilerParams(vmem_limit_bytes=16 * 1024 * 1024),
    )(*mid)


def solution(mesh):
    in_specs = (
        P("row", None),
        P("row", None),
        P("row", None),
        P("row", "col"),
        P("row", "col"),
        P("row", "col"),
        P("row", "col"),
        P("row", "col"),
    )
    out_specs = (P("row", "col"), P("row", "col"), P("row", "col"))
    return jax.shard_map(
        per_device, mesh=mesh, in_specs=in_specs, out_specs=out_specs, check_vma=False
    )
```

```python
import functools

import jax
import jax.numpy as jnp
from jax import lax
from jax.experimental import pallas as pl
from jax.experimental.pallas import tpu as pltpu
from jax.sharding import PartitionSpec as P

MESH = pl.DeviceIdType.MESH
NG = 8
LATE = 2
HEAD = (
    ("a", 0), ("a", 1), ("a", 2), ("a", 3), ("a", 4), ("a", 5),
    ("o", 0), ("o", 1), ("b", 0), ("b", 1), ("a", 6), ("z0", 1),
    ("b", 2), ("z1", 1), ("b", 3), ("b", 4), ("z0", 2), ("c", 0),
    ("a", 7), ("c", 1), ("b", 5), ("b", 6), ("z1", 2), ("c", 2),
    ("z0", 3), ("b", 7), ("c", 3), ("c", 4), ("d", 0), ("d", 1),
    ("z1", 3), ("c", 5), ("c", 6), ("d", 2), ("c", 7), ("l", 0),
    ("d", 3), ("d", 4), ("l", 1), ("s", 0), ("e", 0), ("e", 1),
    ("d", 5), ("d", 6), ("s", 1), ("e", 2),
)
TAIL = (
    (),
    (("d", 7),),
    (("e", 3),),
    (("e", 4),),
    (("e", 5),),
    (("e", 6),),
    (("e", 7),),
    (),
)

def split(v):
    hi = v.astype(jnp.bfloat16)
    return hi, (v - hi.astype(jnp.float32)).astype(jnp.bfloat16)


def dot3(a, b):
    f = functools.partial(jnp.dot, preferred_element_type=jnp.float32)
    return f(a[0], b[0]) + (f(a[0], b[1]) + f(a[1], b[0]))


def panel_product(grid, st, g):
    acc = None
    for p in range(2):
        m = split(grid[g, p].reshape(32 * 16, grid.shape[-1]))
        t = dot3((st[p, 0], st[p, 1]), m)
        acc = t if acc is None else acc + t
    return acc


def finish(out1, out2, upd, grid, st, o1, o2, o3, tail, sem):
    rows = grid.shape[-1]
    done = (NG - 1) * rows
    copies = [
        pltpu.make_async_copy(upd.at[pl.ds(0, done)], o3.at[pl.ds(0, done)], sem.at[0]),
        pltpu.make_async_copy(out1, o1, sem.at[1]),
        pltpu.make_async_copy(out2, o2, sem.at[2]),
    ]
    for c in copies:
        c.start()
    tail[...] = upd[pl.ds(done, rows), :] - panel_product(grid, st, NG - 1).T
    last = pltpu.make_async_copy(tail, o3.at[pl.ds(done, rows)], sem.at[3])
    last.start()
    for c in copies:
        c.wait()
    last.wait()


def kernel(
    a1, a2, cp, pt0, pt1, r1, r2, rest,
    out1, out2, upd, grid, st,
    zb1, zb2, xb1, xb2, sol,
    rsem, ssem, lsem, zrsem, zssem, zlsem, bsem, ready,
):
    rows = pt0.shape[1] // NG
    z = lax.axis_index("row")
    col = lax.axis_index("col")
    y, x, h = col // 8, (col // 2) % 4, col % 2
    oh = 1 - h

    def cid(yy, xx, hh):
        return (yy * 4 + xx) * 2 + hh

    xp = (z, cid(y, (x + 1) % 4, h))
    xm = (z, cid(y, (x + 3) % 4, h))
    yp = (z, cid((y + 1) % 4, x, h))
    ym = (z, cid((y + 3) % 4, x, h))
    zp = ((z + 1) % 8, col)
    zm = ((z + 7) % 8, col)
    sib = (z, cid(y, x, oh))

    def send(src, dst, s, r, dev):
        pltpu.make_async_remote_copy(
            src_ref=src, dst_ref=dst, send_sem=s, recv_sem=r,
            device_id=dev, device_id_type=MESH,
        ).start()

    def take(ref, sem):
        pltpu.make_async_copy(ref, ref, sem).wait()

    panels = (
        (pt0, x, y, xp, xm, yp, ym),
        (pt1, y, x, yp, ym, xp, xm),
    )

    def local_own(g, p):
        pt, a, b = panels[p][:3]
        src = pt.at[:, pl.ds(pl.multiple_of(g * rows, rows), rows)]
        return pltpu.make_async_copy(src, grid.at[g, p, h, b, a], lsem.at[g, p])

    def stage_a(g):
        for p in range(2):
            pt, a, b, ap, am, bp, bm = panels[p]
            src = pt.at[:, pl.ds(pl.multiple_of(g * rows, rows), rows)]
            dst = grid.at[g, p, h, b, a]
            s = ssem.at[g, p]
            send(src, dst, s, rsem.at[g, p, 0], ap)
            send(src, dst, s, rsem.at[g, p, 1], am)
            send(src, dst, s, rsem.at[g, p, 3], bp)
            send(src, dst, s, rsem.at[g, p, 4], bm)

    def stage_b(g):
        for p in range(2):
            pt, a, b, ap, am, bp, bm = panels[p]
            s = ssem.at[g, p]
            for k, da, to, half in ((0, 3, ap, 0), (1, 1, am, 8)):
                ai = (a + da) % 4
                ref = grid.at[g, p, h, b, ai]
                take(ref, rsem.at[g, p, k])
                part = grid.at[g, p, h, b, ai, pl.ds(half, 8)]
                send(part, part, s, rsem.at[g, p, 2], to)
                send(ref, ref, s, rsem.at[g, p, 3], bp)
                send(ref, ref, s, rsem.at[g, p, 4], bm)

    def stage_c(g):
        for p in range(2):
            pt, a, b, ap, am, bp, bm = panels[p]
            s = ssem.at[g, p]
            ref = grid.at[g, p, h, b, (a + 2) % 4]
            take(ref, rsem.at[g, p, 2])
            send(ref, ref, s, rsem.at[g, p, 3], bp)
            send(ref, ref, s, rsem.at[g, p, 4], bm)
            local_own(g, p).wait()
            ref = grid.at[g, p, h, b]
            send(ref, ref, bsem.at[g, p], rsem.at[g, p, 6], sib)

    def stage_d(g):
        for p in range(2):
            pt, a, b, ap, am, bp, bm = panels[p]
            s = ssem.at[g, p]
            for k, db, to in ((3, 3, bp), (4, 1, bm)):
                bi = (b + db) % 4
                ref = grid.at[g, p, h, bi]
                take(ref, rsem.at[g, p, k])
                less, more = ((3, 2), (0, 1))[k - 3]
                sizes = ((1, b == less), (3, b == more), (2, (b != less) & (b != more)))
                for size, mine in sizes if g >= NG - LATE else ((2, None),):
                    at = 0 if k == 3 else 4 - size
                    part = grid.at[g, p, h, bi, pl.ds(at, size)]
                    go = functools.partial(send, part, part, s, rsem.at[g, p, 5], to)
                    go() if mine is None else pl.when(mine)(go)
                send(ref, ref, bsem.at[g, p], rsem.at[g, p, 6], sib)

    def stage_e(g):
        for p in range(2):
            b = panels[p][2]
            ref = grid.at[g, p, h, (b + 2) % 4]
            take(ref, rsem.at[g, p, 5])
            send(ref, ref, bsem.at[g, p], rsem.at[g, p, 6], sib)

    def stage_f(g):
        for p in range(2):
            take(grid.at[g, p, oh], rsem.at[g, p, 6])
        here = pl.ds(pl.multiple_of(g * rows, rows), rows)
        upd[here, :] = upd[here, :] - panel_product(grid, st, g).T

    mcols = pl.ds(pl.multiple_of(h * 256, 256), 256)
    batches = (
        (zb1, (r1, a1.at[:, mcols])),
        (zb2, (r2, cp.at[:, mcols], a2.at[:, mcols])),
    )

    def z_own(bt):
        zb, items = batches[bt]
        for i, src in enumerate(items):
            dst = zb.at[z, i]
            send(src, dst, zssem.at[bt], zrsem.at[bt, 0], zp)
            send(src, dst, zssem.at[bt], zrsem.at[bt, 3], zm)

    def z_local(bt):
        zb, items = batches[bt]
        return [
            pltpu.make_async_copy(src, zb.at[z, i], zlsem.at[bt, i])
            for i, src in enumerate(items)
        ]

    def z_hop(bt, k):
        zb = batches[bt][0]
        for d, to, half, at in ((8 - k, zp, 0, 0), (k, zm, 32, 3)):
            zi = (z + d) % 8
            ref = zb.at[zi]
            take(ref, zrsem.at[bt, at + k - 1])
            if k < 3:
                send(ref, ref, zssem.at[bt], zrsem.at[bt, at + k], to)
            else:
                part = zb.at[zi, :, pl.ds(half, 32)]
                send(part, part, zssem.at[bt], zrsem.at[bt, 6], to)

    def z_last(bt):
        zb = batches[bt][0]
        take(zb.at[(z + 4) % 8], zrsem.at[bt, 6])
        for c in z_local(bt):
            c.wait()
        if bt == 0:
            send(zb1.at[:, pl.ds(1, 1)], xb1, zssem.at[2], zrsem.at[0, 7], sib)
        else:
            send(zb2.at[:, pl.ds(1, 2)], xb2, zssem.at[3], zrsem.at[1, 7], sib)

    def apply(own, other, load):
        here = split(load(h).reshape(256, 256))
        there = split(load(oh).reshape(256, 256))
        return dot3(split(own.reshape(512, 256)), here) + dot3(
            split(other.reshape(512, 256)), there
        )

    def keep(p, s):
        order = [
            (o // 4 % 4 * 4 + o % 4) * 2 + o // 16 if p == 0
            else (o % 4 * 4 + o // 4 % 4) * 2 + o // 16
            for o in range(32)
        ]
        perm = jnp.concatenate([s[c * 16:c * 16 + 16] for c in order], axis=0)
        hi, lo = split(perm.T)
        st[p, 0] = hi
        st[p, 1] = lo

    def solve_first():
        take(xb1, zrsem.at[0, 7])
        s = apply(
            zb1[:, 1], xb1[:, 0], lambda q: zb1[pl.ds(q * 4, 4), 0]
        )
        sol[0] = s.reshape(8, 64, 256)
        out1[...] = sol[0, z]
        keep(0, s)

    def solve_second():
        take(xb2, zrsem.at[1, 7])
        red = zb2[:, 0].reshape(512, 256) - apply(
            zb2[:, 1], xb2[:, 0], lambda q: sol[0, pl.ds(q * 4, 4)]
        )
        sol[1] = red.reshape(8, 64, 256)
        s = apply(
            zb2[:, 2], xb2[:, 1], lambda q: sol[1, pl.ds(q * 4, 4)]
        )
        sol[1] = s.reshape(8, 64, 256)
        out2[...] = sol[1, z]
        keep(1, s)

    def tell(sem, dev):
        pl.semaphore_signal(sem, inc=1, device_id=dev, device_id_type=MESH)

    barrier = pltpu.get_barrier_semaphore()
    for yy, xx in ((y, x + 1), (y, x + 3), (y + 1, x), (y + 3, x)):
        tell(barrier, (z, cid(yy % 4, xx % 4, 0)))
    for zz in (z + 1, z + 7):
        tell(barrier, (zz % 8, cid(y, x, 1)))

    @pl.when(h == 1)
    def _():
        tell(barrier, sib)

    @pl.when(h == 0)
    def _():
        pl.semaphore_wait(barrier, 9)
        tell(ready, sib)

    @pl.when(h == 1)
    def _():
        pl.semaphore_wait(ready, 1)

    def z_ready():
        @pl.when(h == 1)
        def _():
            pl.semaphore_wait(barrier, 4)
            tell(ready, sib)

        @pl.when(h == 0)
        def _():
            pl.semaphore_wait(ready, 1)

    def z_first(bt):
        if bt == 0:
            z_ready()
        z_own(bt)

    stages = {
        "a": stage_a,
        "b": stage_b,
        "c": stage_c,
        "d": stage_d,
        "e": stage_e,
        "o": z_first,
        "l": z_last,
        "s": lambda bt: (solve_first, solve_second)[bt](),
        "z0": lambda k: z_hop(0, k),
        "z1": lambda k: z_hop(1, k),
    }

    def run(steps):
        for name, arg in steps:
            stages[name](arg)

    def local_starts():
        @pl.loop(0, NG)
        def _(g):
            for p in range(2):
                local_own(g, p).start()

        for bt in range(2):
            for c in z_local(bt):
                c.start()
        rest_copy.start()

    rest_copy = pltpu.make_async_copy(rest, upd, zlsem.at[0, 2])
    run(HEAD[:3])
    local_starts()
    run(HEAD[3:])
    rest_copy.wait()

    @pl.loop(0, NG - 1)
    def _(g):
        for k in range(NG - 1):
            if TAIL[k]:
                @pl.when(g == k)
                def _(k=k):
                    run(TAIL[k])

        stage_f(g)

    run(TAIL[NG - 1])

    for p in range(2):
        take(grid.at[NG - 1, p, oh], rsem.at[NG - 1, p, 6])

    def sent(g, p, chunks):
        take(upd.at[pl.ds(0, chunks * rows // 16)], ssem.at[g, p])

    @pl.loop(0, NG)
    def _(g):
        for p in range(2):
            take(grid.at[g, p, h], bsem.at[g, p])

    @pl.loop(0, NG - LATE)
    def _(g):
        for p in range(2):
            sent(g, p, 15)

    for g in range(NG - LATE, NG):
        for p, b in enumerate((y, x)):
            inner = (b == 1) | (b == 2)
            pl.when(inner)(functools.partial(sent, g, p, 16))
            pl.when(jnp.logical_not(inner))(functools.partial(sent, g, p, 14))

    take(zb1.at[pl.ds(0, 7)], zssem.at[0])
    take(zb2.at[pl.ds(0, 7)], zssem.at[1])
    take(xb1, zssem.at[2])
    take(xb2, zssem.at[3])


def per_device(
    inverse_first,
    inverse_second,
    coupling,
    panel_first,
    panel_second,
    rhs_first,
    rhs_second,
    rhs_rest,
):
    rows = rhs_rest.shape[0]
    f32 = jnp.float32
    group = rows // NG
    any_spec = pl.BlockSpec(memory_space=pltpu.HBM)
    vmem_spec = pl.BlockSpec(memory_space=pltpu.VMEM)
    sem = pltpu.SemaphoreType.DMA
    mid = pl.pallas_call(
        kernel,
        out_shape=(
            pltpu.VMEM((64, 256), f32),
            pltpu.VMEM((64, 256), f32),
            pltpu.VMEM((rows, 256), f32),
            pltpu.VMEM((NG, 2, 2, 4, 4, 16, group), f32),
            pltpu.VMEM((2, 2, 256, 512), jnp.bfloat16),
        ),
        in_specs=[any_spec] * 8,
        out_specs=(vmem_spec,) * 5,
        scratch_shapes=[
            pltpu.VMEM((8, 2, 64, 256), f32),
            pltpu.VMEM((8, 3, 64, 256), f32),
            pltpu.VMEM((8, 1, 64, 256), f32),
            pltpu.VMEM((8, 2, 64, 256), f32),
            pltpu.VMEM((2, 8, 64, 256), f32),
            sem((NG, 2, 7)),
            sem((NG, 2)),
            sem((NG, 2)),
            sem((2, 8)),
            sem((4,)),
            sem((2, 3)),
            sem((NG, 2)),
            pltpu.SemaphoreType.REGULAR,
        ],
        compiler_params=pltpu.CompilerParams(
            collective_id=0, has_side_effects=True, vmem_limit_bytes=24 * 1024 * 1024
        ),
    )(
        *(
            pltpu.with_memory_space_constraint(v, pltpu.HBM)
            for v in (
                inverse_first,
                inverse_second,
                coupling,
                panel_first.T,
                panel_second.T,
                rhs_first,
                rhs_second,
                rhs_rest,
            )
        )
    )
    return pl.pallas_call(
        finish,
        out_shape=(
            jax.ShapeDtypeStruct((64, 256), f32),
            jax.ShapeDtypeStruct((64, 256), f32),
            jax.ShapeDtypeStruct((rows, 256), f32),
        ),
        in_specs=[vmem_spec] * 5,
        out_specs=(any_spec,) * 3,
        scratch_shapes=[pltpu.VMEM((group, 256), f32), sem((4,))],
        compiler_params=pltpu.CompilerParams(vmem_limit_bytes=16 * 1024 * 1024),
    )(*mid)


def solution(mesh):
    in_specs = (
        P("row", None),
        P("row", None),
        P("row", None),
        P("row", "col"),
        P("row", "col"),
        P("row", "col"),
        P("row", "col"),
        P("row", "col"),
    )
    out_specs = (P("row", "col"), P("row", "col"), P("row", "col"))
    return jax.shard_map(
        per_device, mesh=mesh, in_specs=in_specs, out_specs=out_specs, check_vma=False
    )
```
